512 devices in a mesh: dp: 8 (over x, core), expert: 64 (over z, y).
Axes of the slice: x: 4, y: 4, z: 16, core: 2. Of those that a mesh axis runs over, the one named last changes fastest.
Arguments:
- scores: int32 [64, 4096], P('expert', 'dp'), may hold values from 0 to 4095
- tokens: bfloat16 [4096, 4096], P('dp', 'expert'), may hold values from -6 to 6
- w_gate: bfloat16 [64, 1536, 4096], P('expert', 'dp'), may hold values from -0.09375 to 0.09375
- w_up: bfloat16 [64, 1536, 4096], P('expert', 'dp'), may hold values from -0.09375 to 0.09375
- w_down: bfloat16 [64, 1536, 4096], P('expert', 'dp'), may hold values from -0.15625 to 0.15625
Outputs:
- mixed: bfloat16 [4096, 4096], P('dp', 'expert')
The draws below stay inside these ranges and needn't reach their ends.
Inputs may be any that keep to these rules, and one draw needn't show every extreme that they name: `scores`: score bins.
All inputs are finite; a program needn't handle non-finite values.
Results may differ from the reference program's by a relative error of at most 0.02.
Values may be sent and summed in bfloat16 or wider, within the bound.
A program may use at most 64 MiB of HBM per device.

```python
import jax
import jax.numpy as jnp
from jax import lax

D = 4096
HW = 1536
LEVELS = 64
EXPERTS = 64
TOKENS = 4096
CAP = 256
N_DP = 8


def place_ends(values, stream_key, low, high):
    longest = values.shape.index(max(values.shape))
    spots = []
    for shift in (0, 1):
        where = [jax.random.randint(jax.random.fold_in(stream_key, axis), (), 0, length) for axis, length in enumerate(values.shape)]
        where[longest] = (where[longest] + shift) % values.shape[longest]
        spots.append(tuple(where))
    return values.at[spots[0]].set(low).at[spots[1]].set(high)


def block_scale(rng, extent, cuts, low, high):
    gain, own = 1.0, jax.random.fold_in(rng, 6)
    for position, blocks in cuts:
        draws = jnp.exp(jax.random.uniform(jax.random.fold_in(own, position), (blocks,), jnp.float32, low / len(cuts), high / len(cuts)))
        gain = gain * jnp.repeat(draws, extent[position] // blocks).reshape([-1 if axis == position else 1 for axis in range(len(extent))])
    return gain


def normal_values(stream_key, dims, deviation, bound, shards=(), held_as=jnp.bfloat16):
    gain = block_scale(stream_key, dims, shards, -0.22, 0.18) if shards else 1.0
    entries = jax.random.normal(stream_key, dims, jnp.float32) * deviation * gain
    return jnp.minimum(jnp.maximum(entries, -bound), bound).astype(held_as)


def setup_inputs(seed: int = 0) -> dict:
    key_list = jax.random.split(jax.random.key(seed), 6)
    scores = place_ends(jax.random.randint(key_list[0], (EXPERTS, TOKENS), 0, LEVELS * LEVELS), jax.random.fold_in(key_list[0], 1), 0, (LEVELS * LEVELS) - 1).astype(jnp.int32)
    tokens = normal_values(key_list[1], (TOKENS, D), 1.0, 6.0, ((0, 8), (1, 64)))
    w_gate = normal_values(key_list[2], (EXPERTS, HW, D), D ** -0.5, 0.09375, ((0, 64), (1, 8)))
    w_up = normal_values(key_list[3], (EXPERTS, HW, D), D ** -0.5, 0.09375, ((0, 64), (1, 8)))
    w_down = normal_values(key_list[4], (EXPERTS, HW, D), HW ** -0.5, 0.15625, ((0, 64), (1, 8)))
    return dict(scores=scores, tokens=tokens, w_gate=w_gate, w_up=w_up, w_down=w_down)


score_step = 1.0 / 512.0


def choose_tokens(expert_scores):
    bin_ids = jnp.arange(LEVELS, dtype=jnp.int32)
    coarse = expert_scores // LEVELS
    fine_bin = expert_scores % LEVELS
    coarse_counts = jnp.sum((coarse[:, None] == bin_ids[None, :]).astype(jnp.int32), axis=0, dtype=jnp.int32)
    above_coarse = (jnp.sum(coarse_counts, dtype=jnp.int32) - jnp.cumsum(coarse_counts, dtype=jnp.int32)).astype(jnp.int32)
    cut_coarse = jnp.sum((above_coarse >= CAP).astype(jnp.int32), dtype=jnp.int32)
    need = (CAP - jnp.sum(jnp.where(bin_ids == cut_coarse, above_coarse, 0), dtype=jnp.int32)).astype(jnp.int32)
    inside = (coarse == cut_coarse)[:, None]
    fine_counts = jnp.sum(((fine_bin[:, None] == bin_ids[None, :]) & inside).astype(jnp.int32), axis=0, dtype=jnp.int32)
    above_fine = (jnp.sum(fine_counts, dtype=jnp.int32) - jnp.cumsum(fine_counts, dtype=jnp.int32)).astype(jnp.int32)
    cut_fine = jnp.sum((above_fine >= need).astype(jnp.int32), dtype=jnp.int32)
    allowed = (need - jnp.sum(jnp.where(bin_ids == cut_fine, above_fine, 0), dtype=jnp.int32)).astype(jnp.int32)
    cutoff = (cut_coarse * LEVELS + cut_fine).astype(jnp.int32)
    tie_mask = (expert_scores == cutoff).astype(jnp.int32)
    tie_rank = (jnp.cumsum(tie_mask, dtype=jnp.int32) - tie_mask).astype(jnp.int32)
    chosen = (expert_scores > cutoff) | ((tie_mask > 0) & (tie_rank < allowed))
    chosen_int = chosen.astype(jnp.int32)
    slot_ids = (jnp.cumsum(chosen_int, dtype=jnp.int32) - chosen_int).astype(jnp.int32)
    slot_dest = jnp.where(chosen, slot_ids, CAP).astype(jnp.int32)
    table = jnp.zeros((CAP,), jnp.int32).at[slot_dest].set(jnp.arange(TOKENS, dtype=jnp.int32), mode="drop")
    return chosen, table


def reference(scores, tokens, w_gate, w_up, w_down):
    chosen, slot_tokens = lax.map(choose_tokens, scores)
    weight = jnp.exp(scores.astype(jnp.float32) * score_step)
    den = jnp.sum(jnp.where(chosen, weight, jnp.float32(0.0)), axis=0)
    slot_weight = jnp.take_along_axis(weight, slot_tokens, axis=1)
    group = HW // N_DP

    def one_expert(total, items):
        table, table_weight, gate_mat, up_mat, down_mat = items
        inputs = tokens[table]
        gate_val = jnp.dot(inputs, gate_mat.T, preferred_element_type=jnp.float32)
        up_val = jnp.dot(inputs, up_mat.T, preferred_element_type=jnp.float32)
        hidden = (jax.nn.silu(gate_val) * up_val).astype(jnp.bfloat16)
        contrib = jnp.zeros((CAP, D), jnp.float32)
        for index in range(N_DP):
            part = jnp.dot(hidden[:, index * group:(index + 1) * group], down_mat[index * group:(index + 1) * group], preferred_element_type=jnp.float32).astype(jnp.bfloat16)
            part = lax.optimization_barrier(part)
            contrib = contrib + part.astype(jnp.float32)
        total = total.at[table].add(contrib * table_weight[:, None])
        return total, None

    total, unused = lax.scan(one_expert, jnp.zeros((TOKENS, D), jnp.float32), (slot_tokens, slot_weight, w_gate, w_up, w_down))
    return (total / jnp.maximum(den, jnp.float32(1.0))[:, None]).astype(jnp.bfloat16)
```

```python
import functools

import jax
import jax.numpy as jnp
from jax import lax
from jax.experimental import pallas as pl
from jax.experimental.pallas import tpu as pltpu
from jax.sharding import PartitionSpec as P

SCORE_BITS = 12
SCORE_STEP = 1.0 / 512.0
MESH = pl.DeviceIdType.MESH
VMEM = pl.BlockSpec(memory_space=pltpu.VMEM)


def params(collective_id):
    return pltpu.CompilerParams(
        collective_id=collective_id, has_side_effects=True, vmem_limit_bytes=48 * 1024 * 1024
    )


def greet(dp_size, exp_size, with_dp, with_expert):
    d, e = lax.axis_index("dp"), lax.axis_index("expert")
    barrier = pltpu.get_barrier_semaphore()
    count = 0
    if with_expert:

        @pl.loop(1, exp_size)
        def _(step):
            pl.semaphore_signal(
                barrier, inc=1, device_id=(d, lax.rem(e + step, exp_size)), device_id_type=MESH
            )

        count += exp_size - 1
    if with_dp:

        @pl.loop(1, dp_size)
        def _(step):
            pl.semaphore_signal(
                barrier, inc=1, device_id=(lax.rem(d + step, dp_size), e), device_id_type=MESH
            )

        count += dp_size - 1
    pl.semaphore_wait(barrier, count)


def select_kernel(capacity, tok_rows, d_ref, scores_ref, out_ref):
    d = d_ref[0]
    scores = scores_ref[...]
    rows, lanes = scores.shape
    cut = jnp.zeros((1, 1), jnp.int32)
    for bit in range(SCORE_BITS - 1, -1, -1):
        trial = cut + (1 << bit)
        count = jnp.sum((scores >= trial).astype(jnp.float32), keepdims=True)
        cut = jnp.where(count >= capacity, trial, cut)
    over = (scores > cut).astype(jnp.float32)
    tie = (scores == cut).astype(jnp.float32)
    allowed = capacity - jnp.sum(over, keepdims=True)
    lane_a = lax.broadcasted_iota(jnp.int32, (lanes, lanes), 0)
    lane_b = lax.broadcasted_iota(jnp.int32, (lanes, lanes), 1)
    before_lane = (lane_a < lane_b).astype(jnp.float32)
    row_a = lax.broadcasted_iota(jnp.int32, (rows, rows), 0)
    row_b = lax.broadcasted_iota(jnp.int32, (rows, rows), 1)
    before_row = (row_b < row_a).astype(jnp.float32)

    def rank(mask):
        in_row = jnp.dot(mask, before_lane, preferred_element_type=jnp.float32)
        totals = jnp.broadcast_to(jnp.sum(mask, axis=1, keepdims=True), (rows, lanes))
        return in_row + jnp.dot(before_row, totals, preferred_element_type=jnp.float32)

    chosen = jnp.maximum(over, jnp.where(rank(tie) < allowed, tie, 0.0))
    picked = chosen > 0.0
    slots = out_slots = capacity * tok_rows // (rows * lanes)
    slot_ids = jnp.where(picked, rank(chosen), -1.0).astype(jnp.int32) - d * slots
    place = lax.broadcasted_iota(jnp.int32, (slots, lanes), 0)
    lane = lax.broadcasted_iota(jnp.int32, (1, lanes), 1)
    kind = lax.broadcasted_iota(jnp.int32, (8, lanes), 0)
    table = jnp.zeros((8, slots), jnp.float32)
    for row in range(rows):
        hit = (slot_ids[row : row + 1, :] == place).astype(jnp.float32)
        score = scores[row : row + 1, :]
        entry = jnp.where(kind == 0, row, 0)
        entry = jnp.where(kind == 1, lane, entry)
        entry = jnp.where(kind == 2, score >> 6, entry)
        entry = jnp.where(kind == 3, score & 63, entry)
        table += lax.dot_general(
            entry.astype(jnp.float32),
            hit,
            (((1,), (1,)), ((), ())),
            preferred_element_type=jnp.float32,
        )
    table = table.astype(jnp.int32)
    per_row = tok_rows // lanes
    masked = jnp.where(picked, scores, -1)
    own = jnp.zeros((per_row, lanes), jnp.int32)
    for step in range(rows // per_row):
        own += jnp.where(d == step, masked[step * per_row : (step + 1) * per_row, :], 0)
    out_ref[...] = jnp.zeros_like(out_ref)
    out_ref[0:per_row, :] = own
    out_ref[per_row : per_row + 1, 0:slots] = table[0:1, :] * lanes + table[1:2, :]
    out_ref[per_row + 1 : per_row + 2, 0:slots] = table[2:3, :] * 64 + table[3:4, :]


def share_kernel(dp_size, exp_size, in_ref, out_ref, local_sem, send_sems, recv_sems):
    d, e = lax.axis_index("dp"), lax.axis_index("expert")
    greet(dp_size, exp_size, False, True)
    own = pltpu.make_async_copy(in_ref, out_ref.at[e], local_sem)
    own.start()

    def copy(step):
        peer = lax.rem(e + step, exp_size)
        return pltpu.make_async_remote_copy(
            src_ref=in_ref,
            dst_ref=out_ref.at[e],
            send_sem=send_sems.at[step],
            recv_sem=recv_sems.at[step],
            device_id=(d, peer),
            device_id_type=MESH,
        )

    @pl.loop(1, exp_size)
    def _(step):
        copy(step).start()

    own.wait()

    @pl.loop(1, exp_size)
    def _(step):
        copy(step).wait()


def swap_start(exp_size, src_ref, dst_ref, local_sem, send_sems, recv_sems):
    d, e = lax.axis_index("dp"), lax.axis_index("expert")
    own = pltpu.make_async_copy(src_ref.at[e], dst_ref.at[e], local_sem)
    own.start()

    def copy(step):
        peer = lax.rem(e + step, exp_size)
        return pltpu.make_async_remote_copy(
            src_ref=src_ref.at[peer],
            dst_ref=dst_ref.at[e],
            send_sem=send_sems.at[step],
            recv_sem=recv_sems.at[step],
            device_id=(d, peer),
            device_id_type=MESH,
        )

    @pl.loop(1, exp_size)
    def _(step):
        copy(step).start()

    own.wait()

    @pl.loop(1, exp_size)
    def _(step):
        copy(step).wait()


def dispatch_kernel(
    dp_size, exp_size, in_ref, out_ref, landed, x_own, local_sem, send_sems, recv_sems, dsend, drecv
):
    d, e = lax.axis_index("dp"), lax.axis_index("expert")
    chip, core = lax.div(d, 2), lax.rem(d, 2)
    chips = dp_size // 2
    greet(dp_size, exp_size, True, True)
    swap_start(exp_size, in_ref, landed, local_sem, send_sems, recv_sems)
    half = landed.shape[1]
    left = lax.broadcasted_iota(jnp.int32, (half, 128), 1) < 64
    for pair in range(exp_size // 2):
        a = landed[2 * pair].astype(jnp.float32)
        b = landed[2 * pair + 1].astype(jnp.float32)
        cols = pl.ds(pair * 128, 128)
        x_own[0:half, cols] = jnp.where(left, a, pltpu.roll(b, 64, 1)).astype(jnp.bfloat16)
        x_own[half : 2 * half, cols] = jnp.where(left, pltpu.roll(a, 64, 1), b).astype(jnp.bfloat16)
    own = pltpu.make_async_copy(x_own, out_ref.at[d], local_sem)
    own.start()

    def across(step):
        return pltpu.make_async_remote_copy(
            src_ref=x_own,
            dst_ref=out_ref.at[d],
            send_sem=dsend.at[step],
            recv_sem=drecv.at[step],
            device_id=(lax.rem(chip + step, chips) * 2 + core, e),
            device_id_type=MESH,
        )

    def beside(step):
        source = lax.rem(chip - step + chips, chips) * 2 + core
        return pltpu.make_async_remote_copy(
            src_ref=x_own if step == 0 else out_ref.at[source],
            dst_ref=out_ref.at[source],
            send_sem=dsend.at[chips + step],
            recv_sem=drecv.at[chips + step],
            device_id=(chip * 2 + 1 - core, e),
            device_id_type=MESH,
        )

    for step in range(1, chips):
        across(step).start()
    beside(0).start()
    for step in range(1, chips):
        across(step).wait_recv()
        beside(step).start()
    for step in range(1, chips):
        across(step).wait_send()
    for step in range(chips):
        beside(step).wait()
    own.wait()


def return_kernel(
    dp_size,
    exp_size,
    in_ref,
    out_ref,
    from_core,
    pair_sum,
    from_chip,
    packed,
    local_sem,
    send_sems,
    recv_sems,
    dsend,
    drecv,
):
    d, e = lax.axis_index("dp"), lax.axis_index("expert")
    chip, core = lax.div(d, 2), lax.rem(d, 2)
    chips = dp_size // 2
    greet(dp_size, exp_size, True, True)

    def beside(step):
        target = lax.rem(chip + step, chips)
        return pltpu.make_async_remote_copy(
            src_ref=in_ref.at[target * 2 + 1 - core],
            dst_ref=from_core.at[step],
            send_sem=dsend.at[chips + step],
            recv_sem=drecv.at[chips + step],
            device_id=(chip * 2 + 1 - core, e),
            device_id_type=MESH,
        )

    def across(step):
        return pltpu.make_async_remote_copy(
            src_ref=pair_sum.at[step],
            dst_ref=from_chip.at[step],
            send_sem=dsend.at[step],
            recv_sem=drecv.at[step],
            device_id=(lax.rem(chip + step, chips) * 2 + core, e),
            device_id_type=MESH,
        )

    order = [2, 1, 3, 0]
    for step in order:
        beside(step).start()
    for step in order[:-1]:
        beside(step).wait_recv()
        mine = in_ref[lax.rem(chip + step, chips) * 2 + core].astype(jnp.float32)
        pair_sum[step] = (mine + from_core[step].astype(jnp.float32)).astype(jnp.bfloat16)
        across(step).start()
    beside(0).wait_recv()
    for step in order[:-1]:
        across(step).wait_recv()
    half = packed.shape[1]
    left = lax.broadcasted_iota(jnp.int32, (half, 128), 1) < 64
    for pair in range(exp_size // 2):
        cols = pl.ds(pair * 128, 128)
        total = in_ref[d, :, cols].astype(jnp.float32) + from_core[0, :, cols].astype(jnp.float32)
        for step in range(1, chips):
            total += from_chip[step, :, cols].astype(jnp.float32)
        a, b = total[0:half], total[half : 2 * half]
        packed[2 * pair] = jnp.where(left, a, pltpu.roll(b, 64, 1)).astype(jnp.bfloat16)
        packed[2 * pair + 1] = jnp.where(left, pltpu.roll(a, 64, 1), b).astype(jnp.bfloat16)
    for step in order[:-1]:
        across(step).wait_send()
    for step in order:
        beside(step).wait_send()
    swap_start(exp_size, packed, out_ref, local_sem, send_sems, recv_sems)


def finish_kernel(dp_size, exp_size, in_ref, den_ref, out_ref, landed, send_sems, recv_sems):
    d, e = lax.axis_index("dp"), lax.axis_index("expert")
    greet(dp_size, exp_size, True, False)

    def copy(step):
        peer = lax.rem(d + step, dp_size)
        return pltpu.make_async_remote_copy(
            src_ref=in_ref.at[peer],
            dst_ref=landed.at[step],
            send_sem=send_sems.at[step],
            recv_sem=recv_sems.at[step],
            device_id=(peer, e),
            device_id_type=MESH,
        )

    for step in range(1, dp_size):
        copy(step).start()
    for step in range(1, dp_size):
        copy(step).wait()
    total = in_ref[d].astype(jnp.float32)
    for step in range(1, dp_size):
        total += landed[step].astype(jnp.float32)
    out_ref[...] = (total / den_ref[...]).astype(jnp.bfloat16)


def project_rows(inputs, weight_rows):
    return lax.dot_general(
        inputs, weight_rows, (((1,), (1,)), ((), ())), preferred_element_type=jnp.float32
    )


def local(capacity, dp_size, exp_size, scores, tokens, w_gate, w_up, w_down):
    tok_rows, block = tokens.shape
    all_tokens = tok_rows * dp_size
    width = block * exp_size
    slots = capacity // dp_size
    half = slots // 2
    dma = pltpu.SemaphoreType.DMA
    d = lax.axis_index("dp")
    all_scores = lax.all_gather(scores[0], "dp", axis=0, tiled=True).reshape(-1, 128)
    gathered = lax.all_gather(tokens, "dp", axis=0, tiled=True)
    block_out = pl.pallas_call(
        functools.partial(select_kernel, capacity, tok_rows),
        out_shape=jax.ShapeDtypeStruct((8, 128), jnp.int32),
        in_specs=[pl.BlockSpec(memory_space=pltpu.SMEM), VMEM],
        out_specs=VMEM,
    )(d.astype(jnp.int32).reshape(1), all_scores)
    tables = pl.pallas_call(
        functools.partial(share_kernel, dp_size, exp_size),
        out_shape=jax.ShapeDtypeStruct((exp_size, 8, 128), jnp.int32),
        in_specs=[VMEM],
        out_specs=VMEM,
        scratch_shapes=[dma, dma((exp_size,)), dma((exp_size,))],
        compiler_params=params(0),
    )(block_out)
    per_row = tok_rows // 128
    masked = tables[:, 0:per_row, :].reshape(exp_size, tok_rows)
    den = jnp.sum(jnp.where(masked >= 0, jnp.exp(masked.astype(jnp.float32) * SCORE_STEP), 0.0), axis=0)
    den = jnp.maximum(den, 1.0)
    slot_tokens = tables[:, per_row, 0:slots]
    slot_weight = jnp.exp(tables[:, per_row + 1, 0:slots].astype(jnp.float32) * SCORE_STEP)
    low, high = gathered[slot_tokens[:, :half]], gathered[slot_tokens[:, half:]]
    outgoing = jnp.concatenate([low, high], axis=-1)
    inputs = pl.pallas_call(
        functools.partial(dispatch_kernel, dp_size, exp_size),
        out_shape=jax.ShapeDtypeStruct((dp_size, slots, width), jnp.bfloat16),
        in_specs=[VMEM],
        out_specs=VMEM,
        scratch_shapes=[
            pltpu.VMEM((exp_size, half, 128), jnp.bfloat16),
            pltpu.VMEM((slots, width), jnp.bfloat16),
            dma,
            dma((exp_size,)),
            dma((exp_size,)),
            dma((dp_size,)),
            dma((dp_size,)),
        ],
        compiler_params=params(1),
    )(outgoing).reshape(capacity, width)
    gate_val = project_rows(inputs, w_gate[0])
    up_val = project_rows(inputs, w_up[0])
    hidden = (jax.nn.silu(gate_val) * up_val).astype(jnp.bfloat16)
    computed = jnp.dot(hidden, w_down[0], preferred_element_type=jnp.float32).astype(jnp.bfloat16)
    returned = pl.pallas_call(
        functools.partial(return_kernel, dp_size, exp_size),
        out_shape=jax.ShapeDtypeStruct((exp_size, half, 128), jnp.bfloat16),
        in_specs=[VMEM],
        out_specs=VMEM,
        scratch_shapes=[
            pltpu.VMEM((dp_size // 2, slots, width), jnp.bfloat16),
            pltpu.VMEM((dp_size // 2, slots, width), jnp.bfloat16),
            pltpu.VMEM((dp_size // 2, slots, width), jnp.bfloat16),
            pltpu.VMEM((exp_size, half, 128), jnp.bfloat16),
            dma,
            dma((exp_size,)),
            dma((exp_size,)),
            dma((dp_size,)),
            dma((dp_size,)),
        ],
        compiler_params=params(2),
    )(computed.reshape(dp_size, slots, width))
    values = jnp.concatenate([returned[:, :, :block], returned[:, :, block:]], axis=1)
    terms = values.astype(jnp.float32) * slot_weight[:, :, None]
    sums = (
        jnp.zeros((all_tokens, block), jnp.float32)
        .at[slot_tokens.reshape(-1)]
        .add(terms.reshape(-1, block))
    ).astype(jnp.bfloat16)
    sums = sums.reshape(dp_size, 2, tok_rows // 2, block)
    sums = jnp.concatenate([sums[:, 0], sums[:, 1]], axis=-1)
    den_pair = jnp.broadcast_to(den.reshape(2, tok_rows // 2, 1), (2, tok_rows // 2, block))
    den_pair = jnp.concatenate([den_pair[0], den_pair[1]], axis=-1)
    mixed = pl.pallas_call(
        functools.partial(finish_kernel, dp_size, exp_size),
        out_shape=jax.ShapeDtypeStruct((tok_rows // 2, 2 * block), jnp.bfloat16),
        in_specs=[VMEM, VMEM],
        out_specs=VMEM,
        scratch_shapes=[
            pltpu.VMEM((dp_size, tok_rows // 2, 2 * block), jnp.bfloat16),
            dma((dp_size,)),
            dma((dp_size,)),
        ],
        compiler_params=params(3),
    )(sums, den_pair)
    return jnp.concatenate([mixed[:, :block], mixed[:, block:]], axis=0)


def solution(mesh):
    dp_size, exp_size = mesh.shape["dp"], mesh.shape["expert"]
    in_specs = (
        P("expert", "dp"),
        P("dp", "expert"),
        P("expert", "dp", None),
        P("expert", "dp", None),
        P("expert", "dp", None),
    )

    def layer(scores, tokens, w_gate, w_up, w_down):
        capacity = 4 * scores.shape[1] // exp_size
        return jax.shard_map(
            functools.partial(local, capacity, dp_size, exp_size),
            mesh=mesh,
            in_specs=in_specs,
            out_specs=P("dp", "expert"),
            check_vma=False,
        )(scores, tokens, w_gate, w_up, w_down)

    return layer
```

```python
import functools

import jax
import jax.numpy as jnp
from jax import lax
from jax.experimental import pallas as pl
from jax.experimental.pallas import tpu as pltpu
from jax.sharding import PartitionSpec as P

SCORE_BITS = 12
SCORE_STEP = 1.0 / 512.0
MESH = pl.DeviceIdType.MESH
VMEM = pl.BlockSpec(memory_space=pltpu.VMEM)


def params(collective_id):
    return pltpu.CompilerParams(
        collective_id=collective_id, has_side_effects=True, vmem_limit_bytes=56 * 1024 * 1024
    )


def hail(dp_size, exp_size):
    d, e = lax.axis_index("dp"), lax.axis_index("expert")
    barrier = pltpu.get_barrier_semaphore()

    @pl.loop(1, dp_size)
    def _(step):
        pl.semaphore_signal(
            barrier, inc=1, device_id=(lax.rem(d + step, dp_size), e), device_id_type=MESH
        )

    @pl.loop(1, exp_size)
    def _(step):
        pl.semaphore_signal(
            barrier, inc=1, device_id=(d, lax.rem(e + step, exp_size)), device_id_type=MESH
        )


def meet(dp_size, exp_size):
    pl.semaphore_wait(pltpu.get_barrier_semaphore(), dp_size + exp_size - 2)


def select(capacity, tok_rows, d, scores, table_ref):
    rows, lanes = scores.shape
    cut = jnp.zeros((1, 1), jnp.int32)
    for bit in range(SCORE_BITS - 1, -1, -1):
        trial = cut + (1 << bit)
        count = jnp.sum((scores >= trial).astype(jnp.float32), keepdims=True)
        cut = jnp.where(count >= capacity, trial, cut)
    over = (scores > cut).astype(jnp.float32)
    tie = (scores == cut).astype(jnp.float32)
    allowed = capacity - jnp.sum(over, keepdims=True)
    lane_a = lax.broadcasted_iota(jnp.int32, (lanes, lanes), 0)
    lane_b = lax.broadcasted_iota(jnp.int32, (lanes, lanes), 1)
    before_lane = (lane_a < lane_b).astype(jnp.float32)
    row_a = lax.broadcasted_iota(jnp.int32, (rows, rows), 0)
    row_b = lax.broadcasted_iota(jnp.int32, (rows, rows), 1)
    before_row = (row_b < row_a).astype(jnp.float32)

    def rank(mask):
        in_row = jnp.dot(mask, before_lane, preferred_element_type=jnp.float32)
        totals = jnp.broadcast_to(jnp.sum(mask, axis=1, keepdims=True), (rows, lanes))
        return in_row + jnp.dot(before_row, totals, preferred_element_type=jnp.float32)

    chosen = jnp.maximum(over, jnp.where(rank(tie) < allowed, tie, 0.0))
    slots = capacity * tok_rows // (rows * lanes)
    slot_ids = jnp.where(chosen > 0.0, rank(chosen), -1.0).astype(jnp.int32) - d * slots
    place = lax.broadcasted_iota(jnp.int32, (slots, lanes), 0)
    lane = lax.broadcasted_iota(jnp.int32, (1, lanes), 1)
    kind = lax.broadcasted_iota(jnp.int32, (8, lanes), 0)
    table = jnp.zeros((8, slots), jnp.float32)
    for row in range(rows):
        hit = (slot_ids[row : row + 1, :] == place).astype(jnp.float32)
        score = scores[row : row + 1, :]
        entry = jnp.where(kind == 0, row, 0)
        entry = jnp.where(kind == 1, lane, entry)
        entry = jnp.where(kind == 2, score >> 6, entry)
        entry = jnp.where(kind == 3, score & 63, entry)
        table += lax.dot_general(
            entry.astype(jnp.float32),
            hit,
            (((1,), (1,)), ((), ())),
            preferred_element_type=jnp.float32,
        )
    table = table.astype(jnp.int32)
    table_ref[...] = jnp.zeros_like(table_ref)
    table_ref[0:1, 0:slots] = table[0:1, :] * lanes + table[1:2, :]
    table_ref[1:2, 0:slots] = table[2:3, :] * 64 + table[3:4, :]


def turn_tables(exp_size, tables_ref, flat, turned):
    for expert in range(exp_size):
        flat[2 * expert : 2 * expert + 2, :] = tables_ref[expert].astype(jnp.float32)
    turned[...] = jnp.transpose(flat[...])


def spread(exp_size, slots, turned, token_of):
    for expert in range(exp_size):
        column = turned[0:slots, 2 * expert : 2 * expert + 1].astype(jnp.int32)
        token_of[expert * slots : (expert + 1) * slots, :] = jnp.broadcast_to(column, (slots, 128))


def one_hot(token_of, first, tok_rows):
    lane = lax.broadcasted_iota(jnp.int32, token_of.shape, 1)
    own = token_of[...] - first
    parts = [
        jnp.where(own == lane + step * 128, 1.0, 0.0).astype(jnp.bfloat16)
        for step in range(tok_rows // 128)
    ]
    return jnp.concatenate(parts, axis=1)


def expert_copy(exp_size, src_of, dst_ref, send_sems, recv_sems):
    d, e = lax.axis_index("dp"), lax.axis_index("expert")

    def copy(step):
        peer = lax.rem(e + step, exp_size)
        return pltpu.make_async_remote_copy(
            src_ref=src_of(peer),
            dst_ref=dst_ref.at[e],
            send_sem=send_sems.at[step],
            recv_sem=recv_sems.at[step],
            device_id=(d, peer),
            device_id_type=MESH,
        )

    return copy


def start_all(copy, size):
    @pl.loop(1, size)
    def _(step):
        copy(step).start()


def wait_all(copy, size):
    @pl.loop(1, size)
    def _(step):
        copy(step).wait()


def dispatch_kernel(
    capacity,
    dp_size,
    exp_size,
    scores_ref,
    tokens_ref,
    out_ref,
    tables_ref,
    scores_all,
    scores_flat,
    tokens_all,
    table_own,
    flat,
    turned,
    token_of,
    picked,
    packed,
    landed,
    x_own,
    ssend,
    srecv,
    tsend,
    trecv,
    send_sems,
    recv_sems,
    send_sems2,
    recv_sems2,
    dsend,
    drecv,
):
    d, e = lax.axis_index("dp"), lax.axis_index("expert")
    chip, core = lax.div(d, 2), lax.rem(d, 2)
    chips = dp_size // 2
    tok_rows = tokens_ref.shape[1]
    slots = capacity // dp_size
    hail(dp_size, exp_size)
    scores_all[d] = scores_ref[...]
    tokens_all[d] = tokens_ref[...]
    meet(dp_size, exp_size)

    def row_copy(src_ref, dst_ref, send, recv):
        def copy(step):
            return pltpu.make_async_remote_copy(
                src_ref=src_ref,
                dst_ref=dst_ref.at[d],
                send_sem=send.at[step],
                recv_sem=recv.at[step],
                device_id=(lax.rem(d + step, dp_size), e),
                device_id_type=MESH,
            )

        return copy

    score_copy = row_copy(scores_ref, scores_all, ssend, srecv)
    token_copy = row_copy(tokens_ref, tokens_all, tsend, trecv)
    start_all(score_copy, dp_size)
    start_all(token_copy, dp_size)
    wait_all(score_copy, dp_size)
    per_row = tok_rows // 128
    for step in range(dp_size):
        scores_flat[step * per_row : (step + 1) * per_row, :] = scores_all[step]
    select(capacity, tok_rows, d, scores_flat[...], table_own)
    tables_ref[e] = table_own[...]
    table_copy = expert_copy(exp_size, lambda peer: table_own, tables_ref, send_sems, recv_sems)
    start_all(table_copy, exp_size)
    wait_all(token_copy, dp_size)
    wait_all(table_copy, exp_size)
    turn_tables(exp_size, tables_ref, flat, turned)
    spread(exp_size, slots, turned, token_of)
    picked[...] = jnp.zeros_like(picked)

    @pl.loop(0, dp_size)
    def _(step):
        rows = tokens_all[step]
        rows = jnp.concatenate([rows, jnp.zeros_like(rows)], axis=0)
        picked[...] += lax.dot_general(
            one_hot(token_of, step * tok_rows, tok_rows),
            rows,
            (((1,), (1,)), ((), ())),
            preferred_element_type=jnp.float32,
        )

    half = slots // 2
    for expert in range(exp_size):
        low = picked[expert * slots : expert * slots + half, :]
        high = picked[expert * slots + half : (expert + 1) * slots, :]
        packed[expert] = (low + pltpu.roll(high, 64, 1)).astype(jnp.bfloat16)
    swap = expert_copy(exp_size, lambda peer: packed.at[peer], landed, send_sems2, recv_sems2)
    start_all(swap, exp_size)
    landed[e] = packed[e]
    wait_all(swap, exp_size)
    left = lax.broadcasted_iota(jnp.int32, (half, 128), 1) < 64
    for pair in range(exp_size // 2):
        a = landed[2 * pair].astype(jnp.float32)
        b = landed[2 * pair + 1].astype(jnp.float32)
        cols = pl.ds(pair * 128, 128)
        x_own[0:half, cols] = jnp.where(left, a, pltpu.roll(b, 64, 1)).astype(jnp.bfloat16)
        x_own[half : 2 * half, cols] = jnp.where(left, pltpu.roll(a, 64, 1), b).astype(jnp.bfloat16)

    def across(step):
        return pltpu.make_async_remote_copy(
            src_ref=x_own,
            dst_ref=out_ref.at[d],
            send_sem=dsend.at[step],
            recv_sem=drecv.at[step],
            device_id=(lax.rem(chip + step, chips) * 2 + core, e),
            device_id_type=MESH,
        )

    def beside(step):
        source = lax.rem(chip - step + chips, chips) * 2 + core
        return pltpu.make_async_remote_copy(
            src_ref=x_own if step == 0 else out_ref.at[source],
            dst_ref=out_ref.at[source],
            send_sem=dsend.at[chips + step],
            recv_sem=drecv.at[chips + step],
            device_id=(chip * 2 + 1 - core, e),
            device_id_type=MESH,
        )

    for step in range(1, chips):
        across(step).start()
    beside(0).start()
    out_ref[d] = x_own[...]
    for step in range(1, chips):
        across(step).wait_recv()
        beside(step).start()
    for step in range(1, chips):
        across(step).wait_send()
    for step in range(chips):
        beside(step).wait()


def return_kernel(
    capacity,
    dp_size,
    exp_size,
    x_ref,
    gate_ref,
    up_ref,
    down_ref,
    tables_ref,
    out_ref,
    part,
    from_core,
    pair_sum,
    from_chip,
    packed,
    landed,
    flat,
    turned,
    token_of,
    hits,
    terms,
    terms_turned,
    outgoing,
    outgoing_den,
    incoming,
    incoming_den,
    send_sems,
    recv_sems,
    dsend,
    drecv,
    fsend,
    frecv,
    gsend,
    grecv,
):
    d, e = lax.axis_index("dp"), lax.axis_index("expert")
    chip, core = lax.div(d, 2), lax.rem(d, 2)
    chips = dp_size // 2
    slots = capacity // dp_size
    tok_rows = out_ref.shape[1]
    width = x_ref.shape[1]
    hail(dp_size, exp_size)
    gate_val = project_rows(x_ref[...], gate_ref[...])
    up_val = project_rows(x_ref[...], up_ref[...])
    hidden = (gate_val / (1.0 + jnp.exp(-gate_val)) * up_val).astype(jnp.bfloat16)
    for step in range(width // 512):
        cols = pl.ds(step * 512, 512)
        product = jnp.dot(hidden, down_ref[:, cols], preferred_element_type=jnp.float32)
        part[:, :, cols] = product.astype(jnp.bfloat16).reshape(dp_size, slots, 512)
    meet(dp_size, exp_size)

    def beside(step):
        target = lax.rem(chip + step, chips)
        return pltpu.make_async_remote_copy(
            src_ref=part.at[target * 2 + 1 - core],
            dst_ref=from_core.at[step],
            send_sem=dsend.at[chips + step],
            recv_sem=drecv.at[chips + step],
            device_id=(chip * 2 + 1 - core, e),
            device_id_type=MESH,
        )

    def across(step):
        return pltpu.make_async_remote_copy(
            src_ref=pair_sum.at[step],
            dst_ref=from_chip.at[step],
            send_sem=dsend.at[step],
            recv_sem=drecv.at[step],
            device_id=(lax.rem(chip + step, chips) * 2 + core, e),
            device_id_type=MESH,
        )

    order = [2, 1, 3, 0]
    for step in order:
        beside(step).start()
    for step in order[:-1]:
        beside(step).wait_recv()
        mine = part[lax.rem(chip + step, chips) * 2 + core].astype(jnp.float32)
        pair_sum[step] = (mine + from_core[step].astype(jnp.float32)).astype(jnp.bfloat16)
        across(step).start()
    turn_tables(exp_size, tables_ref, flat, turned)
    spread(exp_size, slots, turned, token_of)
    beside(0).wait_recv()
    for step in order[:-1]:
        across(step).wait_recv()
    half = packed.shape[1]
    left = lax.broadcasted_iota(jnp.int32, (half, 128), 1) < 64
    for pair in range(exp_size // 2):
        cols = pl.ds(pair * 128, 128)
        total = part[d, :, cols].astype(jnp.float32) + from_core[0, :, cols].astype(jnp.float32)
        for step in range(1, chips):
            total += from_chip[step, :, cols].astype(jnp.float32)
        a, b = total[0:half], total[half : 2 * half]
        packed[2 * pair] = jnp.where(left, a, pltpu.roll(b, 64, 1)).astype(jnp.bfloat16)
        packed[2 * pair + 1] = jnp.where(left, pltpu.roll(a, 64, 1), b).astype(jnp.bfloat16)
    swap = expert_copy(exp_size, lambda peer: packed.at[peer], landed, send_sems, recv_sems)
    start_all(swap, exp_size)
    landed[e] = packed[e]
    for step in order[:-1]:
        across(step).wait_send()
    for step in order:
        beside(step).wait_send()

    @pl.loop(0, dp_size)
    def _(step):
        hits[step] = one_hot(token_of, step * tok_rows, tok_rows)

    wait_all(swap, exp_size)
    lane = lax.broadcasted_iota(jnp.int32, (slots, 128), 1)
    for expert in range(exp_size):
        both = landed[expert].astype(jnp.float32)
        value = jnp.concatenate([both, pltpu.roll(both, 64, 1)], axis=0)
        column = turned[0:slots, 2 * expert + 1 : 2 * expert + 2]
        weight = jnp.exp(jnp.broadcast_to(column, (slots, 128)) * SCORE_STEP)
        value = jnp.where(lane < 64, value * weight, 0.0)
        high = value.astype(jnp.bfloat16).astype(jnp.float32)
        rows = pl.ds(expert * slots, slots)
        terms[rows, 0:128] = high + pltpu.roll(value - high, 64, 1)
        first = weight.astype(jnp.bfloat16).astype(jnp.float32)
        second = (weight - first).astype(jnp.bfloat16).astype(jnp.float32)
        third = weight - first - second
        split = jnp.where(lane == 0, first, jnp.where(lane == 1, second, third))
        terms[rows, 128:256] = jnp.where(lane < 3, split, 0.0)
    terms_turned[...] = jnp.transpose(terms[...]).astype(jnp.bfloat16)

    def sum_copy(step):
        return pltpu.make_async_remote_copy(
            src_ref=outgoing.at[step],
            dst_ref=incoming.at[step],
            send_sem=fsend.at[step],
            recv_sem=frecv.at[step],
            device_id=(lax.rem(d + step, dp_size), e),
            device_id_type=MESH,
        )

    def den_copy(step):
        return pltpu.make_async_remote_copy(
            src_ref=outgoing_den.at[step],
            dst_ref=incoming_den.at[step],
            send_sem=gsend.at[step],
            recv_sem=grecv.at[step],
            device_id=(lax.rem(d + step, dp_size), e),
            device_id_type=MESH,
        )

    def row_sums(step):
        sums = jnp.dot(
            terms_turned[...], hits[lax.rem(d + step, dp_size)], preferred_element_type=jnp.float32
        )
        return sums[0:64] + sums[64:128], jnp.sum(sums[128:136], axis=0, keepdims=True)

    @pl.loop(1, dp_size)
    def _(step):
        sums, den = row_sums(step)
        outgoing[step] = sums.astype(jnp.bfloat16)
        outgoing_den[step] = den
        sum_copy(step).start()
        den_copy(step).start()

    total, den = row_sums(0)
    wait_all(sum_copy, dp_size)
    wait_all(den_copy, dp_size)
    for step in range(1, dp_size):
        total += incoming[step].astype(jnp.float32)
        den += incoming_den[step]
    out_ref[...] = (total / jnp.maximum(den, 1.0)).astype(jnp.bfloat16)


def project_rows(inputs, weight_rows):
    return lax.dot_general(
        inputs, weight_rows, (((1,), (1,)), ((), ())), preferred_element_type=jnp.float32
    )


def local(capacity, dp_size, exp_size, scores, tokens, w_gate, w_up, w_down):
    tok_rows, block = tokens.shape
    width = block * exp_size
    slots = capacity // dp_size
    half = slots // 2
    chips = dp_size // 2
    dma = pltpu.SemaphoreType.DMA
    bf16, f32, i32 = jnp.bfloat16, jnp.float32, jnp.int32
    all_rows = tok_rows * dp_size // 128
    inputs, tables = pl.pallas_call(
        functools.partial(dispatch_kernel, capacity, dp_size, exp_size),
        out_shape=(
            jax.ShapeDtypeStruct((dp_size, slots, width), bf16),
            jax.ShapeDtypeStruct((exp_size, 2, 128), i32),
        ),
        in_specs=[VMEM] * 2,
        out_specs=(VMEM, VMEM),
        scratch_shapes=[
            pltpu.VMEM((dp_size, tok_rows // 128, 128), i32),
            pltpu.VMEM((all_rows, 128), i32),
            pltpu.VMEM((dp_size, block, tok_rows), bf16),
            pltpu.VMEM((2, 128), i32),
            pltpu.VMEM((2 * exp_size, 128), f32),
            pltpu.VMEM((128, 2 * exp_size), f32),
            pltpu.VMEM((exp_size * slots, 128), i32),
            pltpu.VMEM((exp_size * slots, 128), f32),
            pltpu.VMEM((exp_size, half, 128), bf16),
            pltpu.VMEM((exp_size, half, 128), bf16),
            pltpu.VMEM((slots, width), bf16),
            dma((dp_size,)),
            dma((dp_size,)),
            dma((dp_size,)),
            dma((dp_size,)),
            dma((exp_size,)),
            dma((exp_size,)),
            dma((exp_size,)),
            dma((exp_size,)),
            dma((dp_size,)),
            dma((dp_size,)),
        ],
        compiler_params=params(0),
    )(scores.reshape(tok_rows // 128, 128), tokens.T)
    mixed = pl.pallas_call(
        functools.partial(return_kernel, capacity, dp_size, exp_size),
        out_shape=jax.ShapeDtypeStruct((block, tok_rows), bf16),
        in_specs=[VMEM] * 5,
        out_specs=VMEM,
        scratch_shapes=[
            pltpu.VMEM((dp_size, slots, width), bf16),
            pltpu.VMEM((chips, slots, width), bf16),
            pltpu.VMEM((chips, slots, width), bf16),
            pltpu.VMEM((chips, slots, width), bf16),
            pltpu.VMEM((exp_size, half, 128), bf16),
            pltpu.VMEM((exp_size, half, 128), bf16),
            pltpu.VMEM((2 * exp_size, 128), f32),
            pltpu.VMEM((128, 2 * exp_size), f32),
            pltpu.VMEM((exp_size * slots, 128), i32),
            pltpu.VMEM((dp_size, exp_size * slots, tok_rows), bf16),
            pltpu.VMEM((exp_size * slots, 256), f32),
            pltpu.VMEM((256, exp_size * slots), bf16),
            pltpu.VMEM((dp_size, block, tok_rows), bf16),
            pltpu.VMEM((dp_size, 1, tok_rows), f32),
            pltpu.VMEM((dp_size, block, tok_rows), bf16),
            pltpu.VMEM((dp_size, 1, tok_rows), f32),
            dma((exp_size,)),
            dma((exp_size,)),
            dma((dp_size,)),
            dma((dp_size,)),
            dma((dp_size,)),
            dma((dp_size,)),
            dma((dp_size,)),
            dma((dp_size,)),
        ],
        compiler_params=params(1),
    )(inputs.reshape(capacity, width), w_gate[0], w_up[0], w_down[0], tables)
    return mixed.T


def solution(mesh):
    dp_size, exp_size = mesh.shape["dp"], mesh.shape["expert"]
    in_specs = (
        P("expert", "dp"),
        P("dp", "expert"),
        P("expert", "dp", None),
        P("expert", "dp", None),
        P("expert", "dp", None),
    )

    def layer(scores, tokens, w_gate, w_up, w_down):
        capacity = 4 * scores.shape[1] // exp_size
        return jax.shard_map(
            functools.partial(local, capacity, dp_size, exp_size),
            mesh=mesh,
            in_specs=in_specs,
            out_specs=P("dp", "expert"),
            check_vma=False,
        )(scores, tokens, w_gate, w_up, w_down)

    return layer
```

```python
import functools

import jax
import jax.numpy as jnp
from jax import lax
from jax.experimental import pallas as pl
from jax.experimental.pallas import tpu as pltpu
from jax.sharding import PartitionSpec as P

SCORE_BITS = 12
SCORE_STEP = 1.0 / 512.0
MESH = pl.DeviceIdType.MESH
VMEM = pl.BlockSpec(memory_space=pltpu.VMEM)


def params(collective_id):
    return pltpu.CompilerParams(
        collective_id=collective_id, has_side_effects=True, vmem_limit_bytes=56 * 1024 * 1024
    )


def far_first(index, size):
    rank = size - index
    near, odd = lax.div(rank + 1, 2), lax.rem(rank, 2)
    return odd * near + (1 - odd) * (size - near)


def hail(dp_size, exp_size):
    d, e = lax.axis_index("dp"), lax.axis_index("expert")
    barrier = pltpu.get_barrier_semaphore()

    @pl.loop(1, exp_size)
    def _(index):
        peer = lax.rem(e + far_first(index, exp_size), exp_size)
        pl.semaphore_signal(barrier, inc=1, device_id=(d, peer), device_id_type=MESH)

    @pl.loop(1, dp_size)
    def _(step):
        pl.semaphore_signal(
            barrier, inc=1, device_id=(lax.rem(d + step, dp_size), e), device_id_type=MESH
        )


def meet(dp_size, exp_size):
    pl.semaphore_wait(pltpu.get_barrier_semaphore(), dp_size + exp_size - 2)


def select(capacity, tok_rows, d, scores, table_ref):
    rows, lanes = scores.shape
    cut = jnp.zeros((1, 1), jnp.int32)
    for bit in range(SCORE_BITS - 1, -1, -1):
        trial = cut + (1 << bit)
        count = jnp.sum((scores >= trial).astype(jnp.float32), keepdims=True)
        cut = jnp.where(count >= capacity, trial, cut)
    over = (scores > cut).astype(jnp.float32)
    tie = (scores == cut).astype(jnp.float32)
    allowed = capacity - jnp.sum(over, keepdims=True)
    lane_a = lax.broadcasted_iota(jnp.int32, (lanes, lanes), 0)
    lane_b = lax.broadcasted_iota(jnp.int32, (lanes, lanes), 1)
    before_lane = (lane_a < lane_b).astype(jnp.float32)
    row_a = lax.broadcasted_iota(jnp.int32, (rows, rows), 0)
    row_b = lax.broadcasted_iota(jnp.int32, (rows, rows), 1)
    before_row = (row_b < row_a).astype(jnp.float32)

    def rank(mask):
        in_row = jnp.dot(mask, before_lane, preferred_element_type=jnp.float32)
        totals = jnp.broadcast_to(jnp.sum(mask, axis=1, keepdims=True), (rows, lanes))
        return in_row + jnp.dot(before_row, totals, preferred_element_type=jnp.float32)

    chosen = jnp.maximum(over, jnp.where(rank(tie) < allowed, tie, 0.0))
    slots = capacity * tok_rows // (rows * lanes)
    slot_ids = jnp.where(chosen > 0.0, rank(chosen), -1.0).astype(jnp.int32) - d * slots
    place = lax.broadcasted_iota(jnp.int32, (slots, lanes), 0)
    lane = lax.broadcasted_iota(jnp.int32, (1, lanes), 1)
    kind = lax.broadcasted_iota(jnp.int32, (8, lanes), 0)
    table = jnp.zeros((8, slots), jnp.float32)
    for row in range(rows):
        hit = (slot_ids[row : row + 1, :] == place).astype(jnp.float32)
        score = scores[row : row + 1, :]
        entry = jnp.where(kind == 0, row, 0)
        entry = jnp.where(kind == 1, lane, entry)
        entry = jnp.where(kind == 2, score >> 6, entry)
        entry = jnp.where(kind == 3, score & 63, entry)
        table += lax.dot_general(
            entry.astype(jnp.float32),
            hit,
            (((1,), (1,)), ((), ())),
            preferred_element_type=jnp.float32,
        )
    table = table.astype(jnp.int32)
    table_ref[...] = jnp.zeros_like(table_ref)
    table_ref[0:1, 0:slots] = table[0:1, :] * lanes + table[1:2, :]
    table_ref[1:2, 0:slots] = table[2:3, :] * 64 + table[3:4, :]


def turn_tables(exp_size, tables_ref, flat, turned):
    for expert in range(exp_size):
        flat[2 * expert : 2 * expert + 2, :] = tables_ref[expert].astype(jnp.float32)
    turned[...] = jnp.transpose(flat[...])


def spread(exp_size, slots, turned, token_of):
    for expert in range(exp_size):
        column = turned[0:slots, 2 * expert : 2 * expert + 1].astype(jnp.int32)
        token_of[expert * slots : (expert + 1) * slots, :] = jnp.broadcast_to(column, (slots, 128))


def one_hot(token_of, first, tok_rows):
    lane = lax.broadcasted_iota(jnp.int32, token_of.shape, 1)
    own = token_of[...] - first
    parts = [
        jnp.where(own == lane + step * 128, 1.0, 0.0).astype(jnp.bfloat16)
        for step in range(tok_rows // 128)
    ]
    return jnp.concatenate(parts, axis=1)


def expert_copy(exp_size, src_of, dst_ref, send_sems, recv_sems, first=0):
    d, e = lax.axis_index("dp"), lax.axis_index("expert")

    def copy(index):
        step = far_first(index, exp_size)
        peer = lax.rem(e + step, exp_size)
        return pltpu.make_async_remote_copy(
            src_ref=src_of(peer),
            dst_ref=dst_ref.at[e],
            send_sem=send_sems.at[first + step],
            recv_sem=recv_sems.at[first + step],
            device_id=(d, peer),
            device_id_type=MESH,
        )

    return copy


def start_all(copy, size):
    @pl.loop(1, size)
    def _(step):
        copy(step).start()


def wait_all(copy, size):
    @pl.loop(1, size)
    def _(step):
        copy(step).wait()


def dispatch_kernel(
    capacity,
    dp_size,
    exp_size,
    scores_ref,
    tokens_ref,
    out_ref,
    tables_ref,
    scores_all,
    scores_flat,
    tokens_all,
    table_own,
    flat,
    turned,
    token_of,
    picked,
    packed,
    landed,
    x_own,
    ssend,
    srecv,
    tsend,
    trecv,
    send_sems,
    recv_sems,
    send_sems2,
    recv_sems2,
    dsend,
    drecv,
):
    d, e = lax.axis_index("dp"), lax.axis_index("expert")
    chip, core = lax.div(d, 2), lax.rem(d, 2)
    chips = dp_size // 2
    tok_rows = tokens_ref.shape[1]
    slots = capacity // dp_size
    hail(dp_size, exp_size)
    scores_all[d] = scores_ref[...]
    tokens_all[d] = tokens_ref[...]
    meet(dp_size, exp_size)

    def row_copy(src_ref, dst_ref, send, recv):
        def copy(step):
            return pltpu.make_async_remote_copy(
                src_ref=src_ref,
                dst_ref=dst_ref.at[d],
                send_sem=send.at[step],
                recv_sem=recv.at[step],
                device_id=(lax.rem(d + step, dp_size), e),
                device_id_type=MESH,
            )

        return copy

    score_copy = row_copy(scores_ref, scores_all, ssend, srecv)
    token_copy = row_copy(tokens_ref, tokens_all, tsend, trecv)
    start_all(score_copy, dp_size)
    start_all(token_copy, dp_size)
    wait_all(score_copy, dp_size)
    per_row = tok_rows // 128
    for step in range(dp_size):
        scores_flat[step * per_row : (step + 1) * per_row, :] = scores_all[step]
    select(capacity, tok_rows, d, scores_flat[...], table_own)
    tables_ref[e] = table_own[...]
    table_copy = expert_copy(exp_size, lambda peer: table_own, tables_ref, send_sems, recv_sems)
    start_all(table_copy, exp_size)
    wait_all(token_copy, dp_size)
    wait_all(table_copy, exp_size)
    turn_tables(exp_size, tables_ref, flat, turned)
    spread(exp_size, slots, turned, token_of)
    picked[...] = jnp.zeros_like(picked)

    @pl.loop(0, dp_size)
    def _(step):
        rows = tokens_all[step]
        rows = jnp.concatenate([rows, jnp.zeros_like(rows)], axis=0)
        picked[...] += lax.dot_general(
            one_hot(token_of, step * tok_rows, tok_rows),
            rows,
            (((1,), (1,)), ((), ())),
            preferred_element_type=jnp.float32,
        )

    quarter = slots // 4
    swaps = []
    for half in range(2):
        for expert in range(exp_size):
            row = expert * slots + half * 2 * quarter
            low = picked[row : row + quarter, :]
            high = picked[row + quarter : row + 2 * quarter, :]
            packed[half, expert] = (low + pltpu.roll(high, 64, 1)).astype(jnp.bfloat16)
        swap = expert_copy(
            exp_size,
            lambda peer, half=half: packed.at[half, peer],
            landed.at[half],
            send_sems2,
            recv_sems2,
            half * exp_size,
        )
        start_all(swap, exp_size)
        landed[half, e] = packed[half, e]
        swaps.append(swap)

    def across(half, step):
        return pltpu.make_async_remote_copy(
            src_ref=x_own.at[half],
            dst_ref=out_ref.at[d, half],
            send_sem=dsend.at[half * dp_size + step],
            recv_sem=drecv.at[half * dp_size + step],
            device_id=(lax.rem(chip + step, chips) * 2 + core, e),
            device_id_type=MESH,
        )

    def beside(half, step):
        source = lax.rem(chip - step + chips, chips) * 2 + core
        return pltpu.make_async_remote_copy(
            src_ref=x_own.at[half] if step == 0 else out_ref.at[source, half],
            dst_ref=out_ref.at[source, half],
            send_sem=dsend.at[half * dp_size + chips + step],
            recv_sem=drecv.at[half * dp_size + chips + step],
            device_id=(chip * 2 + 1 - core, e),
            device_id_type=MESH,
        )

    left = lax.broadcasted_iota(jnp.int32, (quarter, 128), 1) < 64
    for half in range(2):
        wait_all(swaps[half], exp_size)
        for pair in range(exp_size // 2):
            a = landed[half, 2 * pair].astype(jnp.float32)
            b = landed[half, 2 * pair + 1].astype(jnp.float32)
            first = jnp.where(left, a, pltpu.roll(b, 64, 1))
            second = jnp.where(left, pltpu.roll(a, 64, 1), b)
            rows = jnp.concatenate([first, second], axis=0).astype(jnp.bfloat16)
            x_own[half, :, pl.ds(pair * 128, 128)] = rows
        for step in range(1, chips):
            across(half, step).start()
        beside(half, 0).start()
        out_ref[d, half] = x_own[half]
    for half in range(2):
        for step in range(1, chips):
            across(half, step).wait_recv()
            beside(half, step).start()
    for half in range(2):
        for step in range(1, chips):
            across(half, step).wait_send()
        for step in range(chips):
            beside(half, step).wait()


def return_kernel(
    capacity,
    dp_size,
    exp_size,
    x_ref,
    gate_ref,
    up_ref,
    down_ref,
    tables_ref,
    out_ref,
    part,
    from_core,
    pair_sum,
    from_chip,
    packed,
    landed,
    flat,
    turned,
    token_of,
    hits,
    terms,
    terms_turned,
    outgoing,
    outgoing_den,
    incoming,
    incoming_den,
    send_sems,
    recv_sems,
    dsend,
    drecv,
    fsend,
    frecv,
    gsend,
    grecv,
):
    d, e = lax.axis_index("dp"), lax.axis_index("expert")
    chip, core = lax.div(d, 2), lax.rem(d, 2)
    chips = dp_size // 2
    slots = capacity // dp_size
    tok_rows = out_ref.shape[1]
    width = x_ref.shape[1]
    hail(dp_size, exp_size)
    gate_val = project_rows(x_ref[...], gate_ref[...])
    up_val = project_rows(x_ref[...], up_ref[...])
    hidden = (gate_val / (1.0 + jnp.exp(-gate_val)) * up_val).astype(jnp.bfloat16)
    for step in range(width // 512):
        cols = pl.ds(step * 512, 512)
        product = jnp.dot(hidden, down_ref[:, cols], preferred_element_type=jnp.float32)
        part[:, :, :, cols] = product.astype(jnp.bfloat16).reshape(dp_size, 2, slots // 2, 512)
    meet(dp_size, exp_size)

    def beside(half, step):
        target = lax.rem(chip + step, chips)
        return pltpu.make_async_remote_copy(
            src_ref=part.at[target * 2 + 1 - core, half],
            dst_ref=from_core.at[half, step],
            send_sem=dsend.at[half * dp_size + chips + step],
            recv_sem=drecv.at[half * dp_size + chips + step],
            device_id=(chip * 2 + 1 - core, e),
            device_id_type=MESH,
        )

    def across(half, step):
        return pltpu.make_async_remote_copy(
            src_ref=pair_sum.at[half, step],
            dst_ref=from_chip.at[half, step],
            send_sem=dsend.at[half * dp_size + step],
            recv_sem=drecv.at[half * dp_size + step],
            device_id=(lax.rem(chip + step, chips) * 2 + core, e),
            device_id_type=MESH,
        )

    order = [2, 1, 3, 0]
    for half in range(2):
        for step in order:
            beside(half, step).start()
    for half in range(2):
        for step in order[:-1]:
            beside(half, step).wait_recv()
            mine = part[lax.rem(chip + step, chips) * 2 + core, half].astype(jnp.float32)
            mine += from_core[half, step].astype(jnp.float32)
            pair_sum[half, step] = mine.astype(jnp.bfloat16)
            across(half, step).start()
    turn_tables(exp_size, tables_ref, flat, turned)
    spread(exp_size, slots, turned, token_of)
    quarter = slots // 4
    left = lax.broadcasted_iota(jnp.int32, (quarter, 128), 1) < 64
    swaps = []
    for half in range(2):
        beside(half, 0).wait_recv()
        for step in order[:-1]:
            across(half, step).wait_recv()
        for pair in range(exp_size // 2):
            cols = pl.ds(pair * 128, 128)
            total = part[d, half, :, cols].astype(jnp.float32)
            total += from_core[half, 0, :, cols].astype(jnp.float32)
            for step in range(1, chips):
                total += from_chip[half, step, :, cols].astype(jnp.float32)
            a, b = total[0:quarter], total[quarter : 2 * quarter]
            first = jnp.where(left, a, pltpu.roll(b, 64, 1))
            second = jnp.where(left, pltpu.roll(a, 64, 1), b)
            packed[half, 2 * pair] = first.astype(jnp.bfloat16)
            packed[half, 2 * pair + 1] = second.astype(jnp.bfloat16)
        swap = expert_copy(
            exp_size,
            lambda peer, half=half: packed.at[half, peer],
            landed.at[half],
            send_sems,
            recv_sems,
            half * exp_size,
        )
        start_all(swap, exp_size)
        landed[half, e] = packed[half, e]
        swaps.append(swap)
    for half in range(2):
        for step in order[:-1]:
            across(half, step).wait_send()
        for step in order:
            beside(half, step).wait_send()

    @pl.loop(0, dp_size)
    def _(step):
        hits[step] = one_hot(token_of, step * tok_rows, tok_rows)

    for swap in swaps:
        wait_all(swap, exp_size)
    lane = lax.broadcasted_iota(jnp.int32, (slots, 128), 1)
    for expert in range(exp_size):
        value = []
        for half in range(2):
            both = landed[half, expert].astype(jnp.float32)
            value += [both, pltpu.roll(both, 64, 1)]
        value = jnp.concatenate(value, axis=0)
        column = turned[0:slots, 2 * expert + 1 : 2 * expert + 2]
        weight = jnp.exp(jnp.broadcast_to(column, (slots, 128)) * SCORE_STEP)
        value = jnp.where(lane < 64, value * weight, 0.0)
        high = value.astype(jnp.bfloat16).astype(jnp.float32)
        rows = pl.ds(expert * slots, slots)
        terms[rows, 0:128] = high + pltpu.roll(value - high, 64, 1)
        first = weight.astype(jnp.bfloat16).astype(jnp.float32)
        second = (weight - first).astype(jnp.bfloat16).astype(jnp.float32)
        third = weight - first - second
        split = jnp.where(lane == 0, first, jnp.where(lane == 1, second, third))
        terms[rows, 128:256] = jnp.where(lane < 3, split, 0.0)
    terms_turned[...] = jnp.transpose(terms[...]).astype(jnp.bfloat16)

    def sum_copy(step):
        return pltpu.make_async_remote_copy(
            src_ref=outgoing.at[step],
            dst_ref=incoming.at[step],
            send_sem=fsend.at[step],
            recv_sem=frecv.at[step],
            device_id=(lax.rem(d + step, dp_size), e),
            device_id_type=MESH,
        )

    def den_copy(step):
        return pltpu.make_async_remote_copy(
            src_ref=outgoing_den.at[step],
            dst_ref=incoming_den.at[step],
            send_sem=gsend.at[step],
            recv_sem=grecv.at[step],
            device_id=(lax.rem(d + step, dp_size), e),
            device_id_type=MESH,
        )

    def row_sums(step):
        sums = jnp.dot(
            terms_turned[...], hits[lax.rem(d + step, dp_size)], preferred_element_type=jnp.float32
        )
        return sums[0:64] + sums[64:128], jnp.sum(sums[128:136], axis=0, keepdims=True)

    @pl.loop(1, dp_size)
    def _(step):
        sums, den = row_sums(step)
        outgoing[step] = sums.astype(jnp.bfloat16)
        outgoing_den[step] = den
        sum_copy(step).start()
        den_copy(step).start()

    total, den = row_sums(0)
    wait_all(sum_copy, dp_size)
    wait_all(den_copy, dp_size)
    for step in range(1, dp_size):
        total += incoming[step].astype(jnp.float32)
        den += incoming_den[step]
    out_ref[...] = (total / jnp.maximum(den, 1.0)).astype(jnp.bfloat16)


def project_rows(inputs, weight_rows):
    return lax.dot_general(
        inputs, weight_rows, (((1,), (1,)), ((), ())), preferred_element_type=jnp.float32
    )


def local(capacity, dp_size, exp_size, scores, tokens, w_gate, w_up, w_down):
    tok_rows, block = tokens.shape
    width = block * exp_size
    slots = capacity // dp_size
    half = slots // 2
    chips = dp_size // 2
    dma = pltpu.SemaphoreType.DMA
    bf16, f32, i32 = jnp.bfloat16, jnp.float32, jnp.int32
    all_rows = tok_rows * dp_size // 128
    inputs, tables = pl.pallas_call(
        functools.partial(dispatch_kernel, capacity, dp_size, exp_size),
        out_shape=(
            jax.ShapeDtypeStruct((dp_size, 2, half, width), bf16),
            jax.ShapeDtypeStruct((exp_size, 2, 128), i32),
        ),
        in_specs=[VMEM] * 2,
        out_specs=(VMEM, VMEM),
        scratch_shapes=[
            pltpu.VMEM((dp_size, tok_rows // 128, 128), i32),
            pltpu.VMEM((all_rows, 128), i32),
            pltpu.VMEM((dp_size, block, tok_rows), bf16),
            pltpu.VMEM((2, 128), i32),
            pltpu.VMEM((2 * exp_size, 128), f32),
            pltpu.VMEM((128, 2 * exp_size), f32),
            pltpu.VMEM((exp_size * slots, 128), i32),
            pltpu.VMEM((exp_size * slots, 128), f32),
            pltpu.VMEM((2, exp_size, half // 2, 128), bf16),
            pltpu.VMEM((2, exp_size, half // 2, 128), bf16),
            pltpu.VMEM((2, half, width), bf16),
            dma((dp_size,)),
            dma((dp_size,)),
            dma((dp_size,)),
            dma((dp_size,)),
            dma((exp_size,)),
            dma((exp_size,)),
            dma((2 * exp_size,)),
            dma((2 * exp_size,)),
            dma((2 * dp_size,)),
            dma((2 * dp_size,)),
        ],
        compiler_params=params(0),
    )(scores.reshape(tok_rows // 128, 128), tokens.T)
    mixed = pl.pallas_call(
        functools.partial(return_kernel, capacity, dp_size, exp_size),
        out_shape=jax.ShapeDtypeStruct((block, tok_rows), bf16),
        in_specs=[VMEM] * 5,
        out_specs=VMEM,
        scratch_shapes=[
            pltpu.VMEM((dp_size, 2, half, width), bf16),
            pltpu.VMEM((2, chips, half, width), bf16),
            pltpu.VMEM((2, chips, half, width), bf16),
            pltpu.VMEM((2, chips, half, width), bf16),
            pltpu.VMEM((2, exp_size, half // 2, 128), bf16),
            pltpu.VMEM((2, exp_size, half // 2, 128), bf16),
            pltpu.VMEM((2 * exp_size, 128), f32),
            pltpu.VMEM((128, 2 * exp_size), f32),
            pltpu.VMEM((exp_size * slots, 128), i32),
            pltpu.VMEM((dp_size, exp_size * slots, tok_rows), bf16),
            pltpu.VMEM((exp_size * slots, 256), f32),
            pltpu.VMEM((256, exp_size * slots), bf16),
            pltpu.VMEM((dp_size, block, tok_rows), bf16),
            pltpu.VMEM((dp_size, 1, tok_rows), f32),
            pltpu.VMEM((dp_size, block, tok_rows), bf16),
            pltpu.VMEM((dp_size, 1, tok_rows), f32),
            dma((2 * exp_size,)),
            dma((2 * exp_size,)),
            dma((2 * dp_size,)),
            dma((2 * dp_size,)),
            dma((dp_size,)),
            dma((dp_size,)),
            dma((dp_size,)),
            dma((dp_size,)),
        ],
        compiler_params=params(1),
    )(inputs.reshape(capacity, width), w_gate[0], w_up[0], w_down[0], tables)
    return mixed.T


def solution(mesh):
    dp_size, exp_size = mesh.shape["dp"], mesh.shape["expert"]
    in_specs = (
        P("expert", "dp"),
        P("dp", "expert"),
        P("expert", "dp", None),
        P("expert", "dp", None),
        P("expert", "dp", None),
    )

    def layer(scores, tokens, w_gate, w_up, w_down):
        capacity = 4 * scores.shape[1] // exp_size
        return jax.shard_map(
            functools.partial(local, capacity, dp_size, exp_size),
            mesh=mesh,
            in_specs=in_specs,
            out_specs=P("dp", "expert"),
            check_vma=False,
        )(scores, tokens, w_gate, w_up, w_down)

    return layer
```

```python
import functools

import jax
import jax.numpy as jnp
from jax import lax
from jax.experimental import pallas as pl
from jax.experimental.pallas import tpu as pltpu
from jax.sharding import PartitionSpec as P

SCORE_BITS = 12
SCORE_STEP = 1.0 / 512.0
MESH = pl.DeviceIdType.MESH
VMEM = pl.BlockSpec(memory_space=pltpu.VMEM)


def params(collective_id):
    return pltpu.CompilerParams(
        collective_id=collective_id, has_side_effects=True, vmem_limit_bytes=56 * 1024 * 1024
    )


def far_first(index, size):
    rank = size - index
    near, odd = lax.div(rank + 1, 2), lax.rem(rank, 2)
    return odd * near + (1 - odd) * (size - near)


def hail(dp_size, exp_size):
    d, e = lax.axis_index("dp"), lax.axis_index("expert")
    barrier = pltpu.get_barrier_semaphore()

    @pl.loop(1, exp_size)
    def _(index):
        peer = lax.rem(e + far_first(index, exp_size), exp_size)
        pl.semaphore_signal(barrier, inc=1, device_id=(d, peer), device_id_type=MESH)

    @pl.loop(1, dp_size)
    def _(step):
        pl.semaphore_signal(
            barrier, inc=1, device_id=(lax.rem(d + step, dp_size), e), device_id_type=MESH
        )


def meet(dp_size, exp_size):
    pl.semaphore_wait(pltpu.get_barrier_semaphore(), dp_size + exp_size - 2)


def select(capacity, tok_rows, d, scores, table_ref):
    rows, lanes = scores.shape
    cut = jnp.zeros((1, 1), jnp.int32)
    for bit in range(SCORE_BITS - 1, -1, -1):
        trial = cut + (1 << bit)
        count = jnp.sum((scores >= trial).astype(jnp.float32), keepdims=True)
        cut = jnp.where(count >= capacity, trial, cut)
    over = (scores > cut).astype(jnp.float32)
    tie = (scores == cut).astype(jnp.float32)
    allowed = capacity - jnp.sum(over, keepdims=True)
    lane_a = lax.broadcasted_iota(jnp.int32, (lanes, lanes), 0)
    lane_b = lax.broadcasted_iota(jnp.int32, (lanes, lanes), 1)
    before_lane = (lane_a < lane_b).astype(jnp.float32)
    row_a = lax.broadcasted_iota(jnp.int32, (rows, rows), 0)
    row_b = lax.broadcasted_iota(jnp.int32, (rows, rows), 1)
    before_row = (row_b < row_a).astype(jnp.float32)

    def rank(mask):
        in_row = jnp.dot(mask, before_lane, preferred_element_type=jnp.float32)
        totals = jnp.broadcast_to(jnp.sum(mask, axis=1, keepdims=True), (rows, lanes))
        return in_row + jnp.dot(before_row, totals, preferred_element_type=jnp.float32)

    chosen = jnp.maximum(over, jnp.where(rank(tie) < allowed, tie, 0.0))
    slots = capacity * tok_rows // (rows * lanes)
    slot_ids = jnp.where(chosen > 0.0, rank(chosen), -1.0).astype(jnp.int32) - d * slots
    place = lax.broadcasted_iota(jnp.int32, (slots, lanes), 0)
    lane = lax.broadcasted_iota(jnp.int32, (1, lanes), 1)
    kind = lax.broadcasted_iota(jnp.int32, (8, lanes), 0)
    table = jnp.zeros((8, slots), jnp.float32)
    for row in range(rows):
        hit = (slot_ids[row : row + 1, :] == place).astype(jnp.float32)
        score = scores[row : row + 1, :]
        entry = jnp.where(kind == 0, row, 0)
        entry = jnp.where(kind == 1, lane, entry)
        entry = jnp.where(kind == 2, score >> 6, entry)
        entry = jnp.where(kind == 3, score & 63, entry)
        table += lax.dot_general(
            entry.astype(jnp.float32),
            hit,
            (((1,), (1,)), ((), ())),
            preferred_element_type=jnp.float32,
        )
    table = table.astype(jnp.int32)
    table_ref[...] = jnp.zeros_like(table_ref)
    table_ref[0:1, 0:slots] = table[0:1, :] * lanes + table[1:2, :]
    table_ref[1:2, 0:slots] = table[2:3, :] * 64 + table[3:4, :]


def turn_tables(exp_size, tables_ref, flat, turned):
    for expert in range(exp_size):
        flat[2 * expert : 2 * expert + 2, :] = tables_ref[expert].astype(jnp.float32)
    turned[...] = jnp.transpose(flat[...])


def spread(exp_size, slots, turned, token_of):
    for expert in range(exp_size):
        column = turned[0:slots, 2 * expert : 2 * expert + 1].astype(jnp.int32)
        column = jnp.broadcast_to(column, (slots, 128))
        for half in range(2):
            row = (half * exp_size + expert) * (slots // 2)
            token_of[row : row + slots // 2, :] = column[half * slots // 2 : (half + 1) * slots // 2]


def one_hot(token_of, first, tok_rows):
    lane = lax.broadcasted_iota(jnp.int32, token_of.shape, 1)
    own = token_of - first
    parts = [
        jnp.where(own == lane + step * 128, 1.0, 0.0).astype(jnp.bfloat16)
        for step in range(tok_rows // 128)
    ]
    return jnp.concatenate(parts, axis=1)


def expert_copy(exp_size, src_of, dst_ref, send_sems, recv_sems, first=0):
    d, e = lax.axis_index("dp"), lax.axis_index("expert")

    def copy(index):
        step = far_first(index, exp_size)
        peer = lax.rem(e + step, exp_size)
        return pltpu.make_async_remote_copy(
            src_ref=src_of(peer),
            dst_ref=dst_ref.at[e],
            send_sem=send_sems.at[first + step],
            recv_sem=recv_sems.at[first + step],
            device_id=(d, peer),
            device_id_type=MESH,
        )

    return copy


def start_all(copy, size):
    @pl.loop(1, size)
    def _(step):
        copy(step).start()


def wait_all(copy, size):
    @pl.loop(1, size)
    def _(step):
        copy(step).wait()


def dispatch_kernel(
    capacity,
    dp_size,
    exp_size,
    scores_ref,
    tokens_ref,
    out_ref,
    tables_ref,
    scores_all,
    scores_flat,
    tokens_all,
    table_own,
    flat,
    turned,
    token_of,
    picked,
    packed,
    landed,
    x_own,
    ssend,
    srecv,
    tsend,
    trecv,
    send_sems,
    recv_sems,
    send_sems2,
    recv_sems2,
    dsend,
    drecv,
):
    d, e = lax.axis_index("dp"), lax.axis_index("expert")
    chip, core = lax.div(d, 2), lax.rem(d, 2)
    chips = dp_size // 2
    tok_rows = tokens_ref.shape[1]
    slots = capacity // dp_size
    hail(dp_size, exp_size)
    scores_all[d] = scores_ref[...]
    tokens_all[d] = tokens_ref[...]
    meet(dp_size, exp_size)

    def row_copy(src_ref, dst_ref, send, recv):
        def copy(step):
            return pltpu.make_async_remote_copy(
                src_ref=src_ref,
                dst_ref=dst_ref.at[d],
                send_sem=send.at[step],
                recv_sem=recv.at[step],
                device_id=(lax.rem(d + step, dp_size), e),
                device_id_type=MESH,
            )

        return copy

    score_copy = row_copy(scores_ref, scores_all, ssend, srecv)
    token_copy = row_copy(tokens_ref, tokens_all, tsend, trecv)
    start_all(score_copy, dp_size)
    start_all(token_copy, dp_size)
    wait_all(score_copy, dp_size)
    per_row = tok_rows // 128
    for step in range(dp_size):
        scores_flat[step * per_row : (step + 1) * per_row, :] = scores_all[step]
    select(capacity, tok_rows, d, scores_flat[...], table_own)
    tables_ref[e] = table_own[...]
    table_copy = expert_copy(exp_size, lambda peer: table_own, tables_ref, send_sems, recv_sems)
    start_all(table_copy, exp_size)
    wait_all(token_copy, dp_size)
    wait_all(table_copy, exp_size)
    turn_tables(exp_size, tables_ref, flat, turned)
    spread(exp_size, slots, turned, token_of)
    quarter = slots // 4
    swaps = []
    for half in range(2):
        picked[...] = jnp.zeros_like(picked)
        rows_of = pl.ds(half * picked.shape[0], picked.shape[0])

        @pl.loop(0, dp_size)
        def _(step, rows_of=rows_of):
            rows = tokens_all[step]
            rows = jnp.concatenate([rows, jnp.zeros_like(rows)], axis=0)
            picked[...] += lax.dot_general(
                one_hot(token_of[rows_of, :], step * tok_rows, tok_rows),
                rows,
                (((1,), (1,)), ((), ())),
                preferred_element_type=jnp.float32,
            )

        for expert in range(exp_size):
            row = expert * 2 * quarter
            low = picked[row : row + quarter, :]
            high = picked[row + quarter : row + 2 * quarter, :]
            packed[half, expert] = (low + pltpu.roll(high, 64, 1)).astype(jnp.bfloat16)
        swap = expert_copy(
            exp_size,
            lambda peer, half=half: packed.at[half, peer],
            landed.at[half],
            send_sems2,
            recv_sems2,
            half * exp_size,
        )
        start_all(swap, exp_size)
        landed[half, e] = packed[half, e]
        swaps.append(swap)

    def across(half, step):
        return pltpu.make_async_remote_copy(
            src_ref=x_own.at[half],
            dst_ref=out_ref.at[d, half],
            send_sem=dsend.at[half * dp_size + step],
            recv_sem=drecv.at[half * dp_size + step],
            device_id=(lax.rem(chip + step, chips) * 2 + core, e),
            device_id_type=MESH,
        )

    def beside(half, step):
        source = lax.rem(chip - step + chips, chips) * 2 + core
        return pltpu.make_async_remote_copy(
            src_ref=x_own.at[half] if step == 0 else out_ref.at[source, half],
            dst_ref=out_ref.at[source, half],
            send_sem=dsend.at[half * dp_size + chips + step],
            recv_sem=drecv.at[half * dp_size + chips + step],
            device_id=(chip * 2 + 1 - core, e),
            device_id_type=MESH,
        )

    left = lax.broadcasted_iota(jnp.int32, (quarter, 128), 1) < 64
    for half in range(2):
        wait_all(swaps[half], exp_size)
        for pair in range(exp_size // 2):
            a = landed[half, 2 * pair].astype(jnp.float32)
            b = landed[half, 2 * pair + 1].astype(jnp.float32)
            first = jnp.where(left, a, pltpu.roll(b, 64, 1))
            second = jnp.where(left, pltpu.roll(a, 64, 1), b)
            rows = jnp.concatenate([first, second], axis=0).astype(jnp.bfloat16)
            x_own[half, :, pl.ds(pair * 128, 128)] = rows
        for step in range(1, chips):
            across(half, step).start()
        beside(half, 0).start()
        out_ref[d, half] = x_own[half]
    for half in range(2):
        for step in range(1, chips):
            across(half, step).wait_recv()
            beside(half, step).start()
    for half in range(2):
        for step in range(1, chips):
            across(half, step).wait_send()
        for step in range(chips):
            beside(half, step).wait()


def return_kernel(
    capacity,
    dp_size,
    exp_size,
    x_ref,
    gate_ref,
    up_ref,
    down_ref,
    tables_ref,
    out_ref,
    part,
    from_core,
    pair_sum,
    from_chip,
    packed,
    landed,
    flat,
    turned,
    token_of,
    hits,
    terms,
    terms_turned,
    weight_of,
    outgoing,
    outgoing_den,
    incoming,
    incoming_den,
    send_sems,
    recv_sems,
    dsend,
    drecv,
    fsend,
    frecv,
    gsend,
    grecv,
):
    d, e = lax.axis_index("dp"), lax.axis_index("expert")
    chip, core = lax.div(d, 2), lax.rem(d, 2)
    chips = dp_size // 2
    slots = capacity // dp_size
    tok_rows = out_ref.shape[1]
    width = x_ref.shape[1]
    hail(dp_size, exp_size)
    gate_val = project_rows(x_ref[...], gate_ref[...])
    up_val = project_rows(x_ref[...], up_ref[...])
    hidden = (gate_val / (1.0 + jnp.exp(-gate_val)) * up_val).astype(jnp.bfloat16)
    for step in range(width // 512):
        cols = pl.ds(step * 512, 512)
        product = jnp.dot(hidden, down_ref[:, cols], preferred_element_type=jnp.float32)
        part[:, :, :, cols] = product.astype(jnp.bfloat16).reshape(dp_size, 2, slots // 2, 512)
    meet(dp_size, exp_size)

    def beside(half, step):
        target = lax.rem(chip + step, chips)
        return pltpu.make_async_remote_copy(
            src_ref=part.at[target * 2 + 1 - core, half],
            dst_ref=from_core.at[half, step],
            send_sem=dsend.at[half * dp_size + chips + step],
            recv_sem=drecv.at[half * dp_size + chips + step],
            device_id=(chip * 2 + 1 - core, e),
            device_id_type=MESH,
        )

    def across(half, step):
        return pltpu.make_async_remote_copy(
            src_ref=pair_sum.at[half, step],
            dst_ref=from_chip.at[half, step],
            send_sem=dsend.at[half * dp_size + step],
            recv_sem=drecv.at[half * dp_size + step],
            device_id=(lax.rem(chip + step, chips) * 2 + core, e),
            device_id_type=MESH,
        )

    order = [2, 1, 3, 0]
    for half in range(2):
        for step in order:
            beside(half, step).start()
    for half in range(2):
        for step in order[:-1]:
            beside(half, step).wait_recv()
            mine = part[lax.rem(chip + step, chips) * 2 + core, half].astype(jnp.float32)
            mine += from_core[half, step].astype(jnp.float32)
            pair_sum[half, step] = mine.astype(jnp.bfloat16)
            across(half, step).start()
    turn_tables(exp_size, tables_ref, flat, turned)
    spread(exp_size, slots, turned, token_of)
    quarter = slots // 4
    left = lax.broadcasted_iota(jnp.int32, (quarter, 128), 1) < 64
    swaps = []
    for half in range(2):
        beside(half, 0).wait_recv()
        for step in order[:-1]:
            across(half, step).wait_recv()
        for pair in range(exp_size // 2):
            cols = pl.ds(pair * 128, 128)
            total = part[d, half, :, cols].astype(jnp.float32)
            total += from_core[half, 0, :, cols].astype(jnp.float32)
            for step in range(1, chips):
                total += from_chip[half, step, :, cols].astype(jnp.float32)
            a, b = total[0:quarter], total[quarter : 2 * quarter]
            first = jnp.where(left, a, pltpu.roll(b, 64, 1))
            second = jnp.where(left, pltpu.roll(a, 64, 1), b)
            packed[half, 2 * pair] = first.astype(jnp.bfloat16)
            packed[half, 2 * pair + 1] = second.astype(jnp.bfloat16)
        swap = expert_copy(
            exp_size,
            lambda peer, half=half: packed.at[half, peer],
            landed.at[half],
            send_sems,
            recv_sems,
            half * exp_size,
        )
        start_all(swap, exp_size)
        landed[half, e] = packed[half, e]
        swaps.append(swap)
    for half in range(2):
        for step in order[:-1]:
            across(half, step).wait_send()
        for step in order:
            beside(half, step).wait_send()

    @pl.loop(0, dp_size)
    def _(step):
        hits[step] = one_hot(token_of[...], step * tok_rows, tok_rows)

    lane = lax.broadcasted_iota(jnp.int32, (slots, 128), 1)
    for expert in range(exp_size):
        column = turned[0:slots, 2 * expert + 1 : 2 * expert + 2]
        weight = jnp.exp(jnp.broadcast_to(column, (slots, 128)) * SCORE_STEP)
        first = weight.astype(jnp.bfloat16).astype(jnp.float32)
        second = (weight - first).astype(jnp.bfloat16).astype(jnp.float32)
        third = weight - first - second
        split = jnp.where(lane == 0, first, jnp.where(lane == 1, second, third))
        split = jnp.where(lane < 3, split, 0.0)
        weight = jnp.where(lane < 64, weight, 0.0)
        for half in range(2):
            rows = pl.ds((half * exp_size + expert) * 2 * quarter, 2 * quarter)
            part_rows = slice(half * 2 * quarter, (half + 1) * 2 * quarter)
            weight_of[rows, :] = weight[part_rows]
            terms[rows, 128:256] = split[part_rows]
    count = exp_size * 2 * quarter
    for half in range(2):
        wait_all(swaps[half], exp_size)
        for expert in range(exp_size):
            rows = pl.ds((half * exp_size + expert) * 2 * quarter, 2 * quarter)
            both = landed[half, expert].astype(jnp.float32)
            value = jnp.concatenate([both, pltpu.roll(both, 64, 1)], axis=0) * weight_of[rows, :]
            high = value.astype(jnp.bfloat16).astype(jnp.float32)
            terms[rows, 0:128] = high + pltpu.roll(value - high, 64, 1)
        rows = slice(half * count, (half + 1) * count)
        terms_turned[:, rows] = jnp.transpose(terms[rows, :]).astype(jnp.bfloat16)

    def sum_copy(step):
        return pltpu.make_async_remote_copy(
            src_ref=outgoing.at[step],
            dst_ref=incoming.at[step],
            send_sem=fsend.at[step],
            recv_sem=frecv.at[step],
            device_id=(lax.rem(d + step, dp_size), e),
            device_id_type=MESH,
        )

    def den_copy(step):
        return pltpu.make_async_remote_copy(
            src_ref=outgoing_den.at[step],
            dst_ref=incoming_den.at[step],
            send_sem=gsend.at[step],
            recv_sem=grecv.at[step],
            device_id=(lax.rem(d + step, dp_size), e),
            device_id_type=MESH,
        )

    def row_sums(step):
        sums = jnp.dot(
            terms_turned[...], hits[lax.rem(d + step, dp_size)], preferred_element_type=jnp.float32
        )
        return sums[0:64] + sums[64:128], jnp.sum(sums[128:136], axis=0, keepdims=True)

    @pl.loop(1, dp_size)
    def _(step):
        sums, den = row_sums(step)
        outgoing[step] = sums.astype(jnp.bfloat16)
        outgoing_den[step] = den
        sum_copy(step).start()
        den_copy(step).start()

    total, den = row_sums(0)
    wait_all(sum_copy, dp_size)
    wait_all(den_copy, dp_size)
    for step in range(1, dp_size):
        total += incoming[step].astype(jnp.float32)
        den += incoming_den[step]
    out_ref[...] = (total / jnp.maximum(den, 1.0)).astype(jnp.bfloat16)


def project_rows(inputs, weight_rows):
    return lax.dot_general(
        inputs, weight_rows, (((1,), (1,)), ((), ())), preferred_element_type=jnp.float32
    )


def local(capacity, dp_size, exp_size, scores, tokens, w_gate, w_up, w_down):
    tok_rows, block = tokens.shape
    width = block * exp_size
    slots = capacity // dp_size
    half = slots // 2
    chips = dp_size // 2
    dma = pltpu.SemaphoreType.DMA
    bf16, f32, i32 = jnp.bfloat16, jnp.float32, jnp.int32
    all_rows = tok_rows * dp_size // 128
    inputs, tables = pl.pallas_call(
        functools.partial(dispatch_kernel, capacity, dp_size, exp_size),
        out_shape=(
            jax.ShapeDtypeStruct((dp_size, 2, half, width), bf16),
            jax.ShapeDtypeStruct((exp_size, 2, 128), i32),
        ),
        in_specs=[VMEM] * 2,
        out_specs=(VMEM, VMEM),
        scratch_shapes=[
            pltpu.VMEM((dp_size, tok_rows // 128, 128), i32),
            pltpu.VMEM((all_rows, 128), i32),
            pltpu.VMEM((dp_size, block, tok_rows), bf16),
            pltpu.VMEM((2, 128), i32),
            pltpu.VMEM((2 * exp_size, 128), f32),
            pltpu.VMEM((128, 2 * exp_size), f32),
            pltpu.VMEM((exp_size * slots, 128), i32),
            pltpu.VMEM((exp_size * half, 128), f32),
            pltpu.VMEM((2, exp_size, half // 2, 128), bf16),
            pltpu.VMEM((2, exp_size, half // 2, 128), bf16),
            pltpu.VMEM((2, half, width), bf16),
            dma((dp_size,)),
            dma((dp_size,)),
            dma((dp_size,)),
            dma((dp_size,)),
            dma((exp_size,)),
            dma((exp_size,)),
            dma((2 * exp_size,)),
            dma((2 * exp_size,)),
            dma((2 * dp_size,)),
            dma((2 * dp_size,)),
        ],
        compiler_params=params(0),
    )(scores.reshape(tok_rows // 128, 128), tokens.T)
    mixed = pl.pallas_call(
        functools.partial(return_kernel, capacity, dp_size, exp_size),
        out_shape=jax.ShapeDtypeStruct((block, tok_rows), bf16),
        in_specs=[VMEM] * 5,
        out_specs=VMEM,
        scratch_shapes=[
            pltpu.VMEM((dp_size, 2, half, width), bf16),
            pltpu.VMEM((2, chips, half, width), bf16),
            pltpu.VMEM((2, chips, half, width), bf16),
            pltpu.VMEM((2, chips, half, width), bf16),
            pltpu.VMEM((2, exp_size, half // 2, 128), bf16),
            pltpu.VMEM((2, exp_size, half // 2, 128), bf16),
            pltpu.VMEM((2 * exp_size, 128), f32),
            pltpu.VMEM((128, 2 * exp_size), f32),
            pltpu.VMEM((exp_size * slots, 128), i32),
            pltpu.VMEM((dp_size, exp_size * slots, tok_rows), bf16),
            pltpu.VMEM((exp_size * slots, 256), f32),
            pltpu.VMEM((256, exp_size * slots), bf16),
            pltpu.VMEM((exp_size * slots, 128), f32),
            pltpu.VMEM((dp_size, block, tok_rows), bf16),
            pltpu.VMEM((dp_size, 1, tok_rows), f32),
            pltpu.VMEM((dp_size, block, tok_rows), bf16),
            pltpu.VMEM((dp_size, 1, tok_rows), f32),
            dma((2 * exp_size,)),
            dma((2 * exp_size,)),
            dma((2 * dp_size,)),
            dma((2 * dp_size,)),
            dma((dp_size,)),
            dma((dp_size,)),
            dma((dp_size,)),
            dma((dp_size,)),
        ],
        compiler_params=params(1),
    )(inputs.reshape(capacity, width), w_gate[0], w_up[0], w_down[0], tables)
    return mixed.T


def solution(mesh):
    dp_size, exp_size = mesh.shape["dp"], mesh.shape["expert"]
    in_specs = (
        P("expert", "dp"),
        P("dp", "expert"),
        P("expert", "dp", None),
        P("expert", "dp", None),
        P("expert", "dp", None),
    )

    def layer(scores, tokens, w_gate, w_up, w_down):
        capacity = 4 * scores.shape[1] // exp_size
        return jax.shard_map(
            functools.partial(local, capacity, dp_size, exp_size),
            mesh=mesh,
            in_specs=in_specs,
            out_specs=P("dp", "expert"),
            check_vma=False,
        )(scores, tokens, w_gate, w_up, w_down)

    return layer
```
